32 devices in a mesh: dp: 4 (over z), row: 2 (over x), col: 4 (over y, core).
Axes of the slice: x: 2, y: 2, z: 4, core: 2. Of those that a mesh axis runs over, the one named last changes fastest.
Arguments:
- inputs: bfloat16 [2, 8192, 2048], P(None, ('dp', 'col'), 'row'), may hold values from -6 to 6
- query_weight: bfloat16 [2048, 2048], P(('row', 'dp'), 'col'), may hold values from -0.125 to 0.125
- key_weight: bfloat16 [2048, 256], P(('row', 'dp'), 'col'), may hold values from -0.125 to 0.125
- value_weight: bfloat16 [2048, 256], P(('row', 'dp'), 'col'), may hold values from -0.125 to 0.125
- output_weight: bfloat16 [2048, 2048], P('col', ('row', 'dp')), may hold values from -1.5 to 1.5
- gate_weight: bfloat16 [2048, 5632], P(('row', 'dp'), 'col'), may hold values from -0.125 to 0.125
- up_weight: bfloat16 [2048, 5632], P(('row', 'dp'), 'col'), may hold values from -0.125 to 0.125
- down_weight: bfloat16 [5632, 2048], P('col', ('row', 'dp')), may hold values from -0.078125 to 0.078125
- first_gain: float32 [2048], P('row'), may hold values from 0.1 to 1.9
- second_gain: float32 [2048], P('row'), may hold values from 0.1 to 1.9
- cotangent: float32 [2, 8192, 2048], P(None, ('dp', 'col'), 'row'), may hold values from -6 to 6
Outputs:
- block_out: float32 [2, 8192, 2048], P(None, ('dp', 'col'), 'row')
- input_gradient: float32 [2, 8192, 2048], P(None, ('dp', 'col'), 'row')
- query_gradient: float32 [2048, 2048], P(('row', 'dp'), 'col')
- key_gradient: float32 [2048, 256], P(('row', 'dp'), 'col')
- value_gradient: float32 [2048, 256], P(('row', 'dp'), 'col')
- output_gradient: float32 [2048, 2048], P('col', ('row', 'dp'))
- gate_gradient: float32 [2048, 5632], P(('row', 'dp'), 'col')
- up_gradient: float32 [2048, 5632], P(('row', 'dp'), 'col')
- down_gradient: float32 [5632, 2048], P('col', ('row', 'dp'))
- first_gain_gradient: float32 [2048], P('row')
- second_gain_gradient: float32 [2048], P('row')
The draws below stay inside these ranges and needn't reach their ends.
All inputs are finite; a program needn't handle non-finite values.
Results may differ from the reference program's by a relative error of at most 0.022.
Values may be sent and summed in bfloat16 or wider, within the bound.
A program may use at most 448 MiB of HBM per device.

```python
import math
import jax
import jax.numpy as jnp
from jax import lax

D = 2048
FF = 5632
QH = 32
KVH = 4
HD = 64
SEQ_LEN = 1024
BLOCK = 256
MICRO = 2
TOKENS_MB = 8192


def spiked(array, stream_key, source, target, blocks, factor):
    def block_of(dim):
        return (jnp.arange(array.shape[dim]) // (array.shape[dim] // blocks)).reshape((-1,) + (1,) * (array.ndim - 1 - dim))

    one_side = jax.random.permutation(stream_key, blocks)[block_of(target)]
    far = (block_of(target) + blocks // 2) % blocks
    return jnp.where((block_of(source) == one_side) | (block_of(source) == far), factor * array, array)


def block_scale(key, extent, pieces, low, high):
    def one(position, parts):
        heights = jax.random.uniform(jax.random.fold_in(jax.random.fold_in(key, 6), position), (parts,), jnp.float32, low / len(pieces), high / len(pieces))
        return jnp.repeat(jnp.exp(heights), extent[position] // parts).reshape((-1,) + (1,) * (len(extent) - position - 1))

    loudness = one(*pieces[0])
    for cut in pieces[1:]:
        loudness = loudness * one(*cut)
    return loudness


def normal_values(key, extent, scale, most, pieces=(), held_as=jnp.bfloat16):
    values = jax.random.normal(key, extent, jnp.float32) * scale
    if len(pieces) > 0:
        values = block_scale(key, extent, pieces, -0.22, 0.18) * values
    return jnp.clip(values, min=-most, max=most).astype(held_as)


def heavy_noise(own_key, extent, scale, reach, cuts, heavy, kind=jnp.bfloat16):
    array = scale * jax.random.normal(own_key, extent, jnp.float32)
    if cuts:
        array = array * block_scale(own_key, extent, cuts, -0.22, 0.18)
    return jnp.clip(spiked(array, jax.random.fold_in(own_key, 3), *heavy), -reach, reach).astype(kind)


def setup_inputs(seed: int = 0) -> dict:
    seeds = jax.random.split(jax.random.key(seed), 12)
    inputs = heavy_noise(seeds[0], (MICRO, TOKENS_MB, D), 1.0, 6.0, ((1, 16), (2, 2)), (1, 2, 16, 2.0))
    query_weight = normal_values(seeds[1], (D, QH * HD), D ** -0.5, 0.125, ((0, 8), (1, 4)))
    key_weight = normal_values(seeds[2], (D, KVH * HD), D ** -0.5, 0.125, ((0, 8), (1, 4)))
    value_weight = normal_values(seeds[3], (D, KVH * HD), D ** -0.5, 0.125, ((0, 8), (1, 4)))
    output_weight = normal_values(seeds[4], (QH * HD, D), (max(D // 128, 1)) ** -0.5, 1.5, ((0, 4), (1, 8)))
    gate_weight = normal_values(seeds[5], (D, FF), D ** -0.5, 0.125, ((0, 8), (1, 4)))
    up_weight = normal_values(seeds[6], (D, FF), D ** -0.5, 0.125, ((0, 8), (1, 4)))
    down_weight = normal_values(seeds[7], (FF, D), FF ** -0.5, 0.078125, ((0, 4), (1, 8)))
    first_gain = jnp.clip(1.0 + 0.18 * jax.random.normal(seeds[8], (D,), jnp.float32), 0.1, 1.9)
    second_gain = jnp.clip(1.0 + 0.18 * jax.random.normal(seeds[9], (D,), jnp.float32), 0.1, 1.9)
    cotangent = heavy_noise(seeds[10], (MICRO, TOKENS_MB, D), 1.0, 6.0, ((1, 16), (2, 2)), (1, 2, 16, 2.0), jnp.float32)
    return {"inputs": inputs, "query_weight": query_weight, "key_weight": key_weight, "value_weight": value_weight, "output_weight": output_weight, "gate_weight": gate_weight, "up_weight": up_weight, "down_weight": down_weight, "first_gain": first_gain, "second_gain": second_gain, "cotangent": cotangent}


@jax.custom_vjp
def low(v):
    return lax.optimization_barrier(v.astype(jnp.bfloat16)).astype(jnp.float32)

@jax.custom_vjp
def low_back(v):
    return v

def low_keep(v):
    return (low(v), None)

def low_pass(kept, grad):
    return (grad,)

def back_keep(v):
    return (v, None)

def back_low(kept, grad):
    return (low(grad),)
low.defvjp(low_keep, low_pass)
low_back.defvjp(back_keep, back_low)
EPSILON = 1e-05
THETA = 10000.0
HIGHEST = lax.Precision.HIGHEST

def matmul(left, right):
    return jnp.dot(left, right, precision=HIGHEST)

def rope_tables(length):
    half = HD // 2
    inverse = jnp.exp(-jnp.arange(half, dtype=jnp.float32) * (2.0 * math.log(THETA) / HD))
    angles = jnp.arange(length, dtype=jnp.float32)[:, None] * inverse[None, :]
    cosine = jnp.concatenate([jnp.cos(angles), jnp.cos(angles)], axis=1)
    sine = jnp.concatenate([jnp.sin(angles), jnp.sin(angles)], axis=1)
    return (cosine[:, None, :], sine[:, None, :])

def rotate(value):
    half = value.shape[-1] // 2
    return jnp.concatenate([-value[..., half:], value[..., :half]], axis=-1)

def rms_norm(value, gain):
    scale = lax.rsqrt(lax.optimization_barrier(jnp.mean(value * value, axis=-1, keepdims=True)) + EPSILON)
    return low(value * scale * gain)

def forward(x, wq, wk, wv, wo, wg, wu, wd, gain_one, gain_two):
    length = x.shape[0]
    cosine, sine = rope_tables(length)
    xn = rms_norm(x, gain_one)
    raw = low_back(matmul(xn, jnp.concatenate([wq, wk, wv], axis=1)))
    kv_width = KVH * HD
    queries = raw[:, :D].reshape(length, QH, HD)
    keys = raw[:, D:D + kv_width].reshape(length, KVH, HD)
    values = low(raw[:, D + kv_width:].reshape(length, KVH, HD))
    queries = low(queries * cosine + rotate(queries) * sine)
    keys = low(keys * cosine + rotate(keys) * sine)
    grouped = queries.reshape(length, KVH, QH // KVH, HD)
    scores = jnp.einsum('qcgd,kcd->cgqk', grouped, keys, precision=HIGHEST) * (1.0 / math.sqrt(HD))
    scores = low_back(scores)
    blockid = jnp.arange(length) // BLOCK
    allowed = blockid[None, :] <= blockid[:, None]
    scores = jnp.where(allowed, scores, -jnp.inf)
    probs = low(jax.nn.softmax(scores, axis=-1))
    mixed = jnp.einsum('cgqk,kcd->qcgd', probs, values, precision=HIGHEST).reshape(length, D)
    mixed = low(low_back(mixed))
    h = x + low_back(matmul(mixed, wo))
    hn = rms_norm(h, gain_two)
    both = low_back(matmul(hn, jnp.concatenate([wg, wu], axis=1)))
    hidden = low(jax.nn.silu(both[:, :FF]) * both[:, FF:])
    return h + low_back(matmul(hidden, wd))

def reference(inputs, query_weight, key_weight, value_weight, output_weight, gate_weight, up_weight, down_weight, first_gain, second_gain, cotangent):
    params = (query_weight.astype(jnp.float32), key_weight.astype(jnp.float32), value_weight.astype(jnp.float32), output_weight.astype(jnp.float32), gate_weight.astype(jnp.float32), up_weight.astype(jnp.float32), down_weight.astype(jnp.float32), first_gain.astype(jnp.float32), second_gain.astype(jnp.float32))
    seqs = inputs.astype(jnp.float32).reshape(-1, SEQ_LEN, D)
    tangents = cotangent.astype(jnp.float32).reshape(-1, SEQ_LEN, D)

    def one_sequence(carry, pair):
        x, grad_out = pair
        result, pull = jax.vjp(forward, x, *params)
        grads = pull(grad_out)
        carry = tuple((total + part for total, part in zip(carry, grads[1:])))
        return (carry, (result, grads[0]))
    zeros = tuple((jnp.zeros(p.shape, jnp.float32) for p in params))
    totals, (outs, input_grads) = lax.scan(one_sequence, zeros, (seqs, tangents))
    return (outs.reshape(MICRO, TOKENS_MB, D), input_grads.reshape(MICRO, TOKENS_MB, D), totals[0], totals[1], totals[2], totals[3], totals[4], totals[5], totals[6], totals[7], totals[8])
```

```python
import math

import jax
import jax.numpy as jnp
from jax import lax
from jax.sharding import Mesh
from jax.sharding import PartitionSpec as P

D = 2048
HD = 64
BLOCK = 256
EPSILON = 1e-05
THETA = 10000.0
F32 = jnp.float32
BF16 = jnp.bfloat16


def swap(value, axis):
    return lax.ppermute(value, axis, [(0, 1), (1, 0)])


def pair(value, axis, dim=0):
    return jnp.concatenate([value, swap(value, axis)], axis=dim)


def dot(left, right, lc, rc):
    return lax.dot_general(left, right, (((lc,), (rc,)), ((), ())), preferred_element_type=F32)


def rope_tables(length):
    half = HD // 2
    inverse = jnp.exp(-jnp.arange(half, dtype=F32) * (2.0 * math.log(THETA) / HD))
    angles = jnp.arange(length, dtype=F32)[:, None] * inverse[None, :]
    cosine = jnp.concatenate([jnp.cos(angles), jnp.cos(angles)], axis=1)
    sine = jnp.concatenate([jnp.sin(angles), jnp.sin(angles)], axis=1)
    return (cosine[:, None, :], sine[:, None, :])


def rotate(value):
    half = value.shape[-1] // 2
    return jnp.concatenate([-value[..., half:], value[..., :half]], axis=-1)


def rotate_back(value):
    half = value.shape[-1] // 2
    return jnp.concatenate([value[..., half:], -value[..., :half]], axis=-1)


def score_block(queries, keys, allowed):
    length, kv_heads, _ = keys.shape
    grouped = queries.reshape(length, kv_heads, -1, HD)
    scores = jnp.einsum("qcgd,kcd->cgqk", grouped, keys, preferred_element_type=F32) * (
        1.0 / math.sqrt(HD)
    )
    return (jnp.where(allowed, scores, -jnp.inf), grouped)


def attend(queries, keys, values, allowed):
    scores, grouped = score_block(queries, keys, allowed)
    top = jnp.max(scores, axis=-1, keepdims=True)
    total = jnp.sum(jnp.exp(scores - top), axis=-1, keepdims=True)
    logsum = top + jnp.log(total)
    probs = jnp.exp(scores - logsum).astype(BF16)
    mixed = jnp.einsum("cgqk,kcd->qcgd", probs, values, preferred_element_type=F32)
    return (mixed.reshape(keys.shape[0], -1).astype(BF16), logsum)


def attend_back(queries, keys, values, logsum, d_mixed, allowed):
    length, kv_heads, _ = keys.shape
    scores, grouped = score_block(queries, keys, allowed)
    probs = jnp.exp(scores - logsum)
    d_out = d_mixed.reshape(length, kv_heads, -1, HD)
    d_values = jnp.einsum("cgqk,qcgd->kcd", probs.astype(BF16), d_out, preferred_element_type=F32)
    d_probs = jnp.einsum("qcgd,kcd->cgqk", d_out, values, preferred_element_type=F32)
    delta = jnp.sum(d_probs * probs, axis=-1, keepdims=True)
    d_scores = (probs * (d_probs - delta)).astype(BF16)
    factor = 1.0 / math.sqrt(HD)
    d_queries = jnp.einsum("cgqk,kcd->qcgd", d_scores, keys, preferred_element_type=F32) * factor
    d_keys = jnp.einsum("cgqk,qcgd->kcd", d_scores, grouped, preferred_element_type=F32) * factor
    return (d_queries.reshape(length, -1, HD), d_keys, d_values)


def normalize(value, gain):
    scale = lax.rsqrt(jnp.sum(value * value, axis=1, keepdims=True) / D + EPSILON)
    return ((value * scale * gain).astype(BF16), scale)


def normalize_back(grad, value, scale, gain):
    weighted = grad * gain
    inner = jnp.sum(weighted * value, axis=1, keepdims=True)
    back = scale * weighted - value * (scale * scale * scale) * inner / D
    return (back, jnp.sum(grad * value * scale, axis=0))


def gather(weight, dim):
    return pair(lax.all_gather(weight, "dp", axis=dim, tiled=True), "row", dim)


def scatter(mine, dim):
    return lax.psum_scatter(mine, "dp", scatter_dimension=dim, tiled=True)


def body(
    inputs,
    query_weight,
    key_weight,
    value_weight,
    output_weight,
    gate_weight,
    up_weight,
    down_weight,
    first_gain,
    second_gain,
    cotangent,
):
    row = lax.axis_index("row")
    core = lax.axis_index("core")
    tokens = inputs.shape[1]
    local = inputs.shape[2]
    length = 2 * tokens
    q_width = query_weight.shape[1]
    kv_width = key_weight.shape[1]
    heads = q_width // HD
    kv_heads = kv_width // HD

    def take(value):
        first = lax.dynamic_index_in_dim(value, row, 0, keepdims=False)
        second = lax.dynamic_index_in_dim(value, 1 - row, 0, keepdims=False)
        return first, second

    def in_order(value):
        other = swap(value, "core")
        return jnp.where(
            core == 0,
            jnp.concatenate([value, other], axis=0),
            jnp.concatenate([other, value], axis=0),
        )

    def mine(value):
        return lax.dynamic_slice_in_dim(value, core * tokens, tokens, 0)

    def theirs(value):
        return lax.dynamic_slice_in_dim(value, (1 - core) * tokens, tokens, 0)

    own_x, other_x = take(inputs)
    x = jnp.concatenate([own_x, swap(other_x, "row")], axis=1).astype(F32)
    gains = pair(jnp.stack([first_gain, second_gain]), "row", 1)
    gain_one, gain_two = gains[0], gains[1]

    qkv = gather(jnp.concatenate([query_weight, key_weight, value_weight], axis=1), 0)
    qkv_weights = (qkv, swap(qkv, "y"))
    out = gather(output_weight, 1)
    out_weights = (out, swap(out, "y"))
    gate_full = gather(gate_weight, 0)
    up_full = gather(up_weight, 0)
    down_full = gather(down_weight, 1)

    own_c, other_c = take(cotangent)
    other_c = swap(other_c.astype(BF16), "row")
    grad_out = jnp.concatenate([own_c, other_c.astype(F32)], axis=1)
    gy = jnp.concatenate([own_c.astype(BF16), other_c], axis=1)
    gy_far = pair(swap(gy, "y"), "core")
    gy_near = pair(gy, "core")

    cosine, sine = rope_tables(length)
    blockid = jnp.arange(length) // BLOCK
    allowed = blockid[None, :] <= blockid[:, None]
    xn, scale_one = normalize(x, gain_one)
    xn_full = in_order(xn)
    queries, keys, values = [], [], []
    for weight in qkv_weights:
        raw = dot(xn_full, weight, 1, 0)
        q = raw[:, :q_width].reshape(length, heads, HD)
        k = raw[:, q_width : q_width + kv_width].reshape(length, kv_heads, HD)
        queries.append((q * cosine + rotate(q) * sine).astype(BF16))
        keys.append((k * cosine + rotate(k) * sine).astype(BF16))
        values.append(raw[:, q_width + kv_width :].reshape(length, kv_heads, HD).astype(BF16))
    mixed, logsum = [], []
    for q, k, v in zip(queries, keys, values):
        m, l = attend(q, k, v, allowed)
        mixed.append(m)
        logsum.append(l)
    send = sum(dot(theirs(m), w, 1, 0) for m, w in zip(mixed, out_weights)).astype(BF16)
    kept = sum(dot(mine(m), w, 1, 0) for m, w in zip(mixed, out_weights))
    h = x + kept + swap(send, "core").astype(F32)
    hn, scale_two = normalize(h, gain_two)

    hn_far = pair(swap(hn, "y"), "core")
    hn_near = pair(hn, "core")

    def forward(hidden_in):
        gate = dot(hidden_in, gate_full, 1, 0)
        up = dot(hidden_in, up_full, 1, 0)
        sigma = jax.nn.sigmoid(gate)
        return gate, up, sigma, (gate * sigma * up).astype(BF16)

    def backward(gy_part, gate, up, sigma):
        d_hidden = dot(gy_part, down_full, 1, 1)
        d_gate = d_hidden * up * sigma * (1.0 + gate * (1.0 - sigma))
        d_up = d_hidden * (gate * sigma)
        return d_gate.astype(BF16), d_up.astype(BF16)

    def collect(far, near):
        far_sum = far[:tokens] + swap(far[tokens:].astype(BF16), "core").astype(F32)
        from_far = swap(far_sum.astype(BF16), "y").astype(F32)
        near_sum = near[:tokens] + swap(near[tokens:].astype(BF16), "core").astype(F32)
        return near_sum + from_far

    gate_f, up_f, sigma_f, hidden_f = forward(hn_far)
    gate_n, up_n, sigma_n, hidden_n = forward(hn_near)
    block = h + collect(dot(hidden_f, down_full, 1, 0), dot(hidden_n, down_full, 1, 0))

    d_gate_f, d_up_f = backward(gy_far, gate_f, up_f, sigma_f)
    d_gate_n, d_up_n = backward(gy_near, gate_n, up_n, sigma_n)
    hidden_all = jnp.concatenate([hidden_f, hidden_n], axis=0)
    gy_all = jnp.concatenate([gy_far, gy_near], axis=0)
    hn_all = jnp.concatenate([hn_far, hn_near], axis=0)
    d_gate = jnp.concatenate([d_gate_f, d_gate_n], axis=0)
    d_up = jnp.concatenate([d_up_f, d_up_n], axis=0)

    def row_sum(own, other):
        return (own() + swap(other().astype(BF16), "row").astype(F32)).astype(BF16)

    d_hn = collect(
        dot(d_gate_f, gate_full, 1, 1) + dot(d_up_f, up_full, 1, 1),
        dot(d_gate_n, gate_full, 1, 1) + dot(d_up_n, up_full, 1, 1),
    )
    down_grad = scatter(
        row_sum(
            lambda: dot(hidden_all, gy_all[:, :local], 0, 0),
            lambda: dot(hidden_all, gy_all[:, local:], 0, 0),
        ),
        1,
    )
    gate_grad = scatter(
        row_sum(
            lambda: dot(hn_all[:, :local], d_gate, 0, 0),
            lambda: dot(hn_all[:, local:], d_gate, 0, 0),
        ),
        0,
    )
    up_grad = scatter(
        row_sum(
            lambda: dot(hn_all[:, :local], d_up, 0, 0),
            lambda: dot(hn_all[:, local:], d_up, 0, 0),
        ),
        0,
    )
    back_two, gain_part_two = normalize_back(d_hn, h, scale_two, gain_two)
    d_h = grad_out + back_two
    gh = in_order(d_h.astype(BF16))

    def y_row_sum(own, other, dim):
        total = own() + swap(other().astype(BF16), "y").astype(F32)
        left = lax.slice_in_dim(total, 0, local, axis=dim)
        right = lax.slice_in_dim(total, local, 2 * local, axis=dim)
        return (left + swap(right.astype(BF16), "row").astype(F32)).astype(BF16)

    out_grad = scatter(
        y_row_sum(lambda: dot(mixed[0], gh, 0, 0), lambda: dot(mixed[1], gh, 0, 0), 1), 1
    )
    d_raw = []
    for q, k, v, l, w in zip(queries, keys, values, logsum, out_weights):
        d_mixed = dot(gh, w, 1, 1).astype(BF16)
        d_q, d_k, d_v = attend_back(q, k, v, l, d_mixed, allowed)
        d_q = d_q * cosine + rotate_back(d_q * sine)
        d_k = d_k * cosine + rotate_back(d_k * sine)
        d_raw.append(
            jnp.concatenate(
                [d_q.reshape(length, -1), d_k.reshape(length, -1), d_v.reshape(length, -1)], axis=1
            ).astype(BF16)
        )
    send = sum(dot(theirs(d), w, 1, 1) for d, w in zip(d_raw, qkv_weights)).astype(BF16)
    kept = sum(dot(mine(d), w, 1, 1) for d, w in zip(d_raw, qkv_weights))
    d_xn = kept + swap(send, "core").astype(F32)
    qkv_grad = scatter(
        y_row_sum(lambda: dot(xn_full, d_raw[0], 0, 0), lambda: dot(xn_full, d_raw[1], 0, 0), 0), 0
    )
    back_one, gain_part_one = normalize_back(d_xn, x, scale_one, gain_one)
    input_grad = d_h + back_one

    def give(value):
        own = value[:, :local]
        other = swap(value[:, local:].astype(BF16), "row").astype(F32)
        return jnp.where(row == 0, jnp.stack([own, other]), jnp.stack([other, own]))

    parts = jnp.stack([gain_part_one, gain_part_two])
    parts = parts[:, :local] + swap(parts[:, local:], "row")
    parts = lax.psum(parts, ("dp", "y", "core"))
    qkv_grad = qkv_grad.astype(F32)
    return (
        give(block),
        give(input_grad),
        qkv_grad[:, :q_width],
        qkv_grad[:, q_width : q_width + kv_width],
        qkv_grad[:, q_width + kv_width :],
        out_grad.astype(F32),
        gate_grad.astype(F32),
        up_grad.astype(F32),
        down_grad.astype(F32),
        parts[0],
        parts[1],
    )


def solution(mesh):
    shape = dict(mesh.shape)
    grid = Mesh(
        mesh.devices.reshape(shape["dp"], shape["row"], shape["col"] // 2, 2),
        ("dp", "row", "y", "core"),
    )
    col = ("y", "core")
    stream = P(None, ("dp",) + col, "row")
    tall = P(("row", "dp"), col)
    wide = P(col, ("row", "dp"))
    gain = P("row")
    in_specs = (stream, tall, tall, tall, wide, tall, tall, wide, gain, gain, stream)
    out_specs = (stream, stream, tall, tall, tall, wide, tall, tall, wide, gain, gain)
    return jax.shard_map(body, mesh=grid, in_specs=in_specs, out_specs=out_specs, check_vma=False)
```

```python
import functools
import math

import jax
import jax.numpy as jnp
from jax import lax
from jax.experimental import pallas as pl
from jax.sharding import Mesh
from jax.sharding import PartitionSpec as P


D = 2048
HD = 64
BLOCK = 256
EPSILON = 1e-05
THETA = 10000.0
F32 = jnp.float32
BF16 = jnp.bfloat16


def swap(value, axis):
    return lax.ppermute(value, axis, [(0, 1), (1, 0)])


def pair(value, axis, dim=0):
    return jnp.concatenate([value, swap(value, axis)], axis=dim)


def gather(weight, dim):
    return lax.all_gather(weight, "dp", axis=dim, tiled=True)


def dot(left, right, lc, rc):
    return lax.dot_general(left, right, (((lc,), (rc,)), ((), ())), preferred_element_type=F32)


def rope_tables(length, heads):
    half = HD // 2
    inverse = jnp.exp(-jnp.arange(half, dtype=F32) * (2.0 * math.log(THETA) / HD))
    angles = jnp.arange(length, dtype=F32)[:, None] * inverse[None, :]
    cosine, sine = jnp.cos(angles), jnp.sin(angles)
    return (jnp.tile(cosine, (1, 2 * heads)), jnp.tile(sine, (1, 2 * heads)))


def rotate(value):
    half = HD // 2
    low = lax.broadcasted_iota(jnp.int32, value.shape, 1) % HD < half
    return jnp.where(low, -jnp.roll(value, -half, axis=1), jnp.roll(value, half, axis=1))


def attend(queries, keys, values):
    length, width = queries.shape
    blocks = length // BLOCK
    pairs = width // (2 * HD)

    def kernel(q_ref, k_ref, vt_ref, o_ref, l_ref):
        block = pl.program_id(1)

        def run(count):
            k = k_ref[: count * BLOCK, :]
            vt = vt_ref[:, : count * BLOCK]
            outs = []
            for head in range(2):
                q = q_ref[:, head * HD : (head + 1) * HD]
                s = dot(k, q, 1, 1)
                top = jnp.max(s, axis=0, keepdims=True)
                p = jnp.exp(s - top)
                total = jnp.sum(p, axis=0, keepdims=True)
                outs.append(dot(vt, p.astype(BF16), 1, 0) / total)
                l_ref[0, head : head + 1, :] = top + jnp.log(total)
            o_ref[...] = jnp.concatenate(outs, axis=0).T.astype(BF16)

        for count in range(1, blocks + 1):
            pl.when(block == count - 1)(functools.partial(run, count))

    part = pl.BlockSpec((BLOCK, 2 * HD), lambda p, b: (b, p))
    return pl.pallas_call(
        kernel,
        grid=(pairs, blocks),
        in_specs=[
            part,
            pl.BlockSpec((length, HD), lambda p, b: (0, 0)),
            pl.BlockSpec((HD, length), lambda p, b: (0, 0)),
        ],
        out_specs=[part, pl.BlockSpec((1, 2, BLOCK), lambda p, b: (p, 0, b))],
        out_shape=[
            jax.ShapeDtypeStruct((length, width), BF16),
            jax.ShapeDtypeStruct((pairs, 2, length), F32),
        ],
        cost_estimate=pl.CostEstimate(
            flops=10 * length * length * width,
            bytes_accessed=6 * length * width,
            transcendentals=length * length * width // HD,
        ),
        name="attend",
    )(queries, keys, values.T)


def attend_back(queries, keys, values, logsum, d_mixed):
    length, width = queries.shape
    blocks = length // BLOCK
    pairs = width // (2 * HD)

    def kernel(q_ref, g_ref, l_ref, k_ref, kt_ref, v_ref, dq_ref, dk_ref, dv_ref):
        block = pl.program_id(1)

        @pl.when((pl.program_id(0) == 0) & (block == 0))
        def _():
            dk_ref[...] = jnp.zeros_like(dk_ref)
            dv_ref[...] = jnp.zeros_like(dv_ref)

        def run(count):
            rows = count * BLOCK
            k, v, kt = k_ref[:rows, :], v_ref[:rows, :], kt_ref[:, :rows]
            qs, gs, ps, ds, outs = [], [], [], [], []
            for head in range(2):
                q = q_ref[:, head * HD : (head + 1) * HD]
                g = g_ref[:, head * HD : (head + 1) * HD]
                p = jnp.exp(dot(k, q, 1, 1) - l_ref[0, head : head + 1, :])
                d_p = dot(v, g, 1, 1)
                delta = jnp.sum(d_p * p, axis=0, keepdims=True)
                d_s = (p * (d_p - delta)).astype(BF16)
                outs.append(dot(kt, d_s, 1, 0) * (1.0 / math.sqrt(HD)))
                qs.append(q)
                gs.append(g)
                ps.append(p.astype(BF16))
                ds.append(d_s)
            dq_ref[...] = jnp.concatenate(outs, axis=0).T
            dv_ref[:rows, :] += dot(
                jnp.concatenate(ps, axis=1), jnp.concatenate(gs, axis=0), 1, 0
            )
            dk_ref[:rows, :] += dot(
                jnp.concatenate(ds, axis=1), jnp.concatenate(qs, axis=0), 1, 0
            )

        for count in range(1, blocks + 1):
            pl.when(block == count - 1)(functools.partial(run, count))

    part = pl.BlockSpec((BLOCK, 2 * HD), lambda p, b: (b, p))
    whole = pl.BlockSpec((length, HD), lambda p, b: (0, 0))
    return pl.pallas_call(
        kernel,
        grid=(pairs, blocks),
        in_specs=[
            part,
            part,
            pl.BlockSpec((1, 2, BLOCK), lambda p, b: (p, 0, b)),
            whole,
            pl.BlockSpec((HD, length), lambda p, b: (0, 0)),
            whole,
        ],
        out_specs=[part, whole, whole],
        out_shape=[
            jax.ShapeDtypeStruct((length, width), F32),
            jax.ShapeDtypeStruct((length, HD), F32),
            jax.ShapeDtypeStruct((length, HD), F32),
        ],
        cost_estimate=pl.CostEstimate(
            flops=25 * length * length * width,
            bytes_accessed=12 * length * width,
            transcendentals=length * length * width // HD,
        ),
        name="attend_back",
    )(queries, d_mixed, logsum, keys, keys.T, values)


def normalize(value, gain):
    scale = lax.rsqrt(jnp.sum(value * value, axis=1, keepdims=True) / D + EPSILON)
    return ((value * scale * gain).astype(BF16), scale)


def normalize_back(grad, value, scale, gain):
    weighted = grad * gain
    inner = jnp.sum(weighted * value, axis=1, keepdims=True)
    back = scale * weighted - value * (scale * scale * scale) * inner / D
    return (back, jnp.sum(grad * value * scale, axis=0))


def tie(*values):
    return lax.optimization_barrier(values)


def scatter(mine, dim):
    return lax.psum_scatter(mine, "dp", scatter_dimension=dim, tiled=True)


def body(
    inputs,
    query_weight,
    key_weight,
    value_weight,
    output_weight,
    gate_weight,
    up_weight,
    down_weight,
    first_gain,
    second_gain,
    cotangent,
):
    row = lax.axis_index("row")
    core = lax.axis_index("core")
    tokens = inputs.shape[1]
    local = inputs.shape[2]
    length = 2 * tokens
    q_width = query_weight.shape[1]
    kv_width = key_weight.shape[1]

    def take(value):
        first = lax.dynamic_index_in_dim(value, row, 0, keepdims=False)
        second = lax.dynamic_index_in_dim(value, 1 - row, 0, keepdims=False)
        return first, second

    def in_order(value):
        other = swap(value, "core")
        return jnp.where(
            core == 0,
            jnp.concatenate([value, other], axis=0),
            jnp.concatenate([other, value], axis=0),
        )

    def mine(value):
        return lax.dynamic_slice_in_dim(value, core * tokens, tokens, 0)

    def theirs(value):
        return lax.dynamic_slice_in_dim(value, (1 - core) * tokens, tokens, 0)

    own_x, other_x = take(inputs)
    x = jnp.concatenate([own_x, swap(other_x, "row")], axis=1).astype(F32)
    gains = pair(jnp.stack([first_gain, second_gain]), "row", 1)
    gain_one, gain_two = gains[0], gains[1]
    own_c, other_c = take(cotangent)
    other_c = other_c.astype(BF16)

    xn, scale_one = normalize(x, gain_one)
    down_weight, xn = tie(down_weight, xn)
    qkv = gather(jnp.concatenate([query_weight, key_weight, value_weight], axis=1), 0)
    out = gather(output_weight, 1)
    gate_part = gather(gate_weight, 0)
    up_part = gather(up_weight, 0)
    down_part = gather(down_weight, 1)
    qkv_own = pair(qkv, "row", 0)
    qkv_y = pair(swap(qkv, "y"), "row", 0)
    out_weights = (pair(out, "row", 1), pair(swap(out, "y"), "row", 1))
    gate_full = pair(gate_part, "row", 0)
    up_full = pair(up_part, "row", 0)
    down_full = pair(down_part, "row", 1)

    roped = q_width + kv_width
    cosine, sine = rope_tables(length, roped // HD)
    xn_full = in_order(xn)
    queries, keys, values, mixed, logsum = [], [], [], [], []
    for group, weight in enumerate((qkv_own, qkv_y)):
        if group:
            weight, mixed[0] = tie(weight, mixed[0])
            qkv_y = weight
        raw = dot(xn_full, weight, 1, 0)
        if not queries:
            raw, other_c = tie(raw, other_c)
            other_c = swap(other_c, "row")
            gy = jnp.concatenate([own_c.astype(BF16), other_c], axis=1)
        else:
            raw, gy = tie(raw, gy)
        both = raw[:, :roped]
        both = (both * cosine + rotate(both) * sine).astype(BF16)
        queries.append(both[:, :q_width] * jnp.bfloat16(1.0 / math.sqrt(HD)))
        keys.append(both[:, q_width:])
        values.append(raw[:, roped:].astype(BF16))
        m, l = attend(queries[-1], keys[-1], values[-1])
        mixed.append(m)
        logsum.append(l)
    grad_out = jnp.concatenate([own_c, other_c.astype(F32)], axis=1)
    qkv_weights = (qkv_own, qkv_y)
    send = sum(dot(theirs(m), w, 1, 0) for m, w in zip(mixed, out_weights)).astype(BF16)
    kept = sum(dot(mine(m), w, 1, 0) for m, w in zip(mixed, out_weights))
    h = x + kept + swap(send, "core").astype(F32)
    hn, scale_two = normalize(h, gain_two)

    def quad(value):
        far = swap(value, "y")
        return jnp.concatenate([value, swap(value, "core"), far, swap(far, "core")], axis=0)

    hn_all = quad(hn)
    gy_all = quad(gy)
    gate = dot(hn_all, gate_full, 1, 0)
    up_full, gate = tie(up_full, gate)
    up = dot(hn_all, up_full, 1, 0)
    sigma = jax.nn.sigmoid(gate)
    hidden = (gate * sigma * up).astype(BF16)
    gy_all, down_full, hidden = tie(gy_all, down_full, hidden)
    d_hidden = dot(gy_all, down_full, 1, 1)
    d_gate = (d_hidden * up * sigma * (1.0 + gate * (1.0 - sigma))).astype(BF16)
    d_up = (d_hidden * (gate * sigma)).astype(BF16)

    def near_sum(part):
        return part[:tokens] + swap(part[tokens:].astype(BF16), "core").astype(F32)

    def hn_back(start):
        rows = slice(start, start + length)
        return dot(d_gate[rows], gate_full, 1, 1) + dot(d_up[rows], up_full, 1, 1)

    d_hn_far = near_sum(hn_back(length)).astype(BF16)
    hidden, d_hn_far = tie(hidden, d_hn_far)
    d_hn_far = swap(d_hn_far, "y")
    down_send = dot(hidden, gy_all[:, local:], 0, 0).astype(BF16)
    d_gate, down_send = tie(d_gate, down_send)
    down_send = swap(down_send, "row")
    gate_send = dot(hn_all[:, local:], d_gate, 0, 0).astype(BF16)
    d_up, gate_send = tie(d_up, gate_send)
    up_send = dot(hn_all[:, local:], d_up, 0, 0).astype(BF16)
    d_gate, d_up, up_send = tie(d_gate, d_up, up_send)
    d_hn = near_sum(hn_back(0))
    gate_send, d_hn = tie(gate_send, d_hn)
    gate_send = swap(gate_send, "row")
    d_hn = d_hn + d_hn_far.astype(F32)
    back_two, gain_part_two = normalize_back(d_hn, h, scale_two, gain_two)
    d_h = grad_out + back_two
    gh_own = d_h.astype(BF16)
    hidden, gh_own = tie(hidden, gh_own)
    gh = in_order(gh_own)
    block_far = near_sum(dot(hidden[length:], down_full, 1, 0)).astype(BF16)
    gh, block_far = tie(gh, block_far)
    block_far = swap(block_far, "y")

    def accumulate(left, right, received):
        return (dot(left, right, 0, 0) + received.astype(F32)).astype(BF16)

    def row_scatter(total, dim):
        left = lax.slice_in_dim(total, 0, local, axis=dim)
        right = lax.slice_in_dim(total, local, 2 * local, axis=dim)
        left = left.astype(F32) + swap(right.astype(BF16), "row").astype(F32)
        return scatter(left.astype(BF16), dim)

    def back_attention(group, gh):
        d_mixed = dot(gh, out_weights[group], 1, 1).astype(BF16)
        d_q, d_k, d_v = attend_back(
            queries[group], keys[group], values[group], logsum[group], d_mixed
        )
        both = jnp.concatenate([d_q, d_k], axis=1)
        both = both * cosine - rotate(both * sine)
        return jnp.concatenate([both, d_v], axis=1).astype(BF16)

    out_send = dot(mixed[1], gh, 0, 0).astype(BF16)
    gh, out_send = tie(gh, out_send)
    out_send = swap(out_send, "y")
    d_raw_other = back_attention(1, gh)
    qkv_send = dot(xn_full, d_raw_other, 0, 0).astype(BF16)
    hidden, qkv_send = tie(hidden, qkv_send)
    qkv_send = swap(qkv_send, "y")
    down_grad = scatter(accumulate(hidden, gy_all[:, :local], down_send), 1)
    gh, hidden, up_send = tie(gh, hidden, up_send)
    up_send = swap(up_send, "row")
    d_raw_own = back_attention(0, gh)
    d_raws = (d_raw_own, d_raw_other)
    send = sum(dot(theirs(d), w, 1, 1) for d, w in zip(d_raws, qkv_weights)).astype(BF16)
    kept = sum(dot(mine(d), w, 1, 1) for d, w in zip(d_raws, qkv_weights))
    d_xn = kept + swap(send, "core").astype(F32)
    back_one, gain_part_one = normalize_back(d_xn, x, scale_one, gain_one)
    input_grad = d_h + back_one
    out_grad = row_scatter(dot(mixed[0], gh, 0, 0) + out_send.astype(F32), 1)
    gate_grad = scatter(accumulate(hn_all[:, :local], d_gate, gate_send), 0)
    up_grad = scatter(accumulate(hn_all[:, :local], d_up, up_send), 0)
    qkv_grad = row_scatter(dot(xn_full, d_raw_own, 0, 0) + qkv_send.astype(F32), 0)
    block = (
        h + near_sum(dot(hidden[:length], down_full, 1, 0)) + block_far.astype(F32)
    )

    def give(value):
        own = value[:, :local]
        other = swap(value[:, local:].astype(BF16), "row").astype(F32)
        return jnp.where(row == 0, jnp.stack([own, other]), jnp.stack([other, own]))

    parts = jnp.stack([gain_part_one, gain_part_two])
    parts = jnp.where(row == 0, parts, jnp.roll(parts, local, axis=1))
    parts = lax.psum(parts, ("dp", "row", "y", "core"))
    parts = lax.dynamic_slice_in_dim(parts, row * local, local, 1)
    qkv_grad = qkv_grad.astype(F32)
    return (
        give(block),
        give(input_grad),
        qkv_grad[:, :q_width],
        qkv_grad[:, q_width : q_width + kv_width],
        qkv_grad[:, q_width + kv_width :],
        out_grad.astype(F32),
        gate_grad.astype(F32),
        up_grad.astype(F32),
        down_grad.astype(F32),
        parts[0],
        parts[1],
    )


def solution(mesh):
    shape = dict(mesh.shape)
    grid = Mesh(
        mesh.devices.reshape(shape["dp"], shape["row"], shape["col"] // 2, 2),
        ("dp", "row", "y", "core"),
    )
    col = ("y", "core")
    stream = P(None, ("dp",) + col, "row")
    tall = P(("row", "dp"), col)
    wide = P(col, ("row", "dp"))
    gain = P("row")
    in_specs = (stream, tall, tall, tall, wide, tall, tall, wide, gain, gain, stream)
    out_specs = (stream, stream, tall, tall, tall, wide, tall, tall, wide, gain, gain)

    return jax.shard_map(body, mesh=grid, in_specs=in_specs, out_specs=out_specs, check_vma=False)
```
